768 devices in a mesh: pb: 16 (over x, z_hi), ga: 48 (over z_lo, y, core).
Axes of the slice: x: 4, y: 8, z: 12 (z_hi: 4, z_lo: 3; z = z_hi * 3 + z_lo), core: 2. Of those that a mesh axis runs over, the one named last changes fastest.
Arguments:
- valence: bfloat16 [96, 16, 16, 4608], P('pb', None, None, 'ga'), may hold values from -6 to 6
- conduction: bfloat16 [96, 16, 8, 4608], P('pb', None, None, 'ga'), may hold values from -6 to 6
- screened: bfloat16 [16, 4608, 4608], P('pb', 'ga'), as said below
- kq_table: int32 [96, 16], P('pb'), may hold values from 0 to 15, each once within a row
Outputs:
- kernel: float32 [96, 16, 8, 16], P('pb')
The draws below stay inside these ranges and needn't reach their ends.
Inputs may be any that keep to these rules, and one draw needn't show every extreme that they name: screened is symmetric in its last two dimensions: screened[q, G, H] = screened[q, H, G] exactly. Each row of kq_table names every label of 0 to 15 once.
All inputs are finite; a program needn't handle non-finite values.
Results may differ from the reference program's by a relative error of at most 0.0003.
Values may be sent and summed in bfloat16 or wider, within the bound.
A program may use at most 128 MiB of HBM per device.

```python
import math
import jax
import jax.numpy as jnp
from jax import lax

NPV = 16
NPC = 8
NG = 4608
NK = 96
NQ = 16


def draw_screened(key, part):
    key_raw = jax.random.fold_in(key, 11)
    key_diag = jax.random.fold_in(key, 12)
    key_scale = jax.random.fold_in(key, 13)
    raw = jnp.clip(jax.random.normal(key_raw, (NQ, NG, NG), jnp.float32), -4.0, 4.0)
    scales = jnp.exp(jax.random.uniform(key_scale, (NQ, NG), jnp.float32, math.log(0.7), math.log(1.4)))
    diag_vals = jnp.exp(jax.random.uniform(key_diag, (NQ, NG), jnp.float32, 0.0, math.log(4.0))) / math.sqrt(NG)
    sym_part = 0.5 * (raw + jnp.swapaxes(raw, 1, 2)) / NG
    row_ids = jnp.arange(NG)[:, None]
    col_ids = jnp.arange(NG)[None, :]
    core = jnp.where(row_ids == col_ids, diag_vals[:, :, None], sym_part)
    outer = scales[:, :, None] * scales[:, None, :]
    return (outer * core).astype(jnp.bfloat16)


def block_scale(key, shape, shards, least, top_value):
    gain = 1.0
    for axis_at, parts in shards:
        steps = jax.random.uniform(jax.random.fold_in(jax.random.fold_in(key, 6), axis_at), (parts,), jnp.float32, least / len(shards), top_value / len(shards))
        gain = gain * jnp.repeat(jnp.exp(steps), shape[axis_at] // parts).reshape((-1,) + (1,) * (len(shape) - 1 - axis_at))
    return gain


def centred(own_key, shape, width, most, cuts=(), kind=jnp.bfloat16):
    array = width * jax.random.normal(own_key, shape, jnp.float32)
    if cuts:
        array = array * block_scale(own_key, shape, cuts, -0.22, 0.18)
    return jnp.clip(array, -most, most).astype(kind)


def setup_inputs(seed: int = 0) -> dict:
    key_of = jax.random.split(jax.random.key(seed), 5)
    valence = centred(key_of[0], (NK, NQ, NPV, NG), 1.0, 6.0, ((0, 16), (3, 48)))
    conduction = centred(key_of[1], (NK, NQ, NPC, NG), 1.0, 6.0, ((0, 16), (3, 48)))
    screened = draw_screened(jax.random.fold_in(key_of[4], 71), 0)
    kq_table = jax.vmap(lambda own: jax.random.permutation(own, NQ))(jax.random.split(key_of[3], NK)).reshape((NK, NQ)).astype(jnp.int32)
    return {"valence": valence, "conduction": conduction, "screened": screened, "kq_table": kq_table}


def one_point(operands):
    w_rows, val_part, con_part = operands
    applied = jnp.einsum("gh,kvh->kvg", w_rows.astype(jnp.float32), val_part.astype(jnp.float32), precision=lax.Precision.HIGHEST)
    return jnp.einsum("kcg,kvg->kcv", con_part.astype(jnp.float32), applied, precision=lax.Precision.HIGHEST)


def reference(valence, conduction, screened, kq_table):
    blocks = lax.map(one_point, (screened, jnp.moveaxis(valence, 1, 0), jnp.moveaxis(conduction, 1, 0)))
    blocks = jnp.moveaxis(blocks, 0, 1)
    k_rows = jnp.arange(NK, dtype=jnp.int32)[:, None]
    kernel = jnp.zeros((NK, NQ, NPC, NPV), jnp.float32).at[k_rows, kq_table].set(blocks)
    return kernel
```

```python
import functools

import jax
import jax.numpy as jnp
from jax import lax
from jax.experimental import pallas as pl
from jax.experimental.pallas import tpu as pltpu
from jax.sharding import PartitionSpec as P

MESH = pl.DeviceIdType.MESH
X, ZH, ZL, Y, CORES = 4, 4, 3, 8, 2
NP, NJ = X * ZH, ZL * Y * CORES
ORDER = (0, 1, 3, 2)
REACH_UP = (4, 3, 3, 4)
REACH_DOWN = (3, 4, 4, 3)
SEQUENCE = tuple(
    item
    for place in range(len(ORDER) + 1)
    for item in (
        ([(ORDER[place], 0)] if place < len(ORDER) else [])
        + ([(ORDER[place - 1], z) for z in range(1, ZL)] if place else [])
    )
)


def kernel(
    val_ref, con_ref, w_ref, table_ref, out_ref,
    con_in, val_in, wide, right, wt, acc, part, tiles, total, back, label,
    con_sem, val_sem, hop_sem, pair_sem, tile_sem, back_sem, sent_sem,
):
    me_p, me_j = lax.axis_index("pb"), lax.axis_index("ga")
    x, zh = me_p // ZH, lax.rem(me_p, ZH)
    zl, y, core = me_j // (Y * CORES), lax.rem(me_j // CORES, Y), lax.rem(me_j, CORES)
    nk, _, npc, own = con_ref.shape
    npv = val_ref.shape[2]
    rows = nk * npc

    def p_of(px, pz):
        return px * ZH + lax.rem(pz, ZH)

    def j_of(jz, jy, jc):
        return (lax.rem(jz, ZL) * Y + lax.rem(jy, Y)) * CORES + jc

    def slot_of(sy, sc, sz, n):
        return ((lax.rem(sy, Y) * CORES + sc) * ZL + lax.rem(sz, ZL)) * ZH + n

    def send(src, dst, sent, arrived, p, j):
        pltpu.make_async_remote_copy(
            src_ref=src, dst_ref=dst, send_sem=sent, recv_sem=arrived, device_id=(p, j), device_id_type=MESH
        ).start()

    def wait(ref, sem):
        pltpu.make_async_copy(ref, ref, sem).wait()

    barrier = pltpu.get_barrier_semaphore()
    peers = [(p_of(lax.rem(x + dx, X), zh + dz), me_j) for dz in range(ZH) for dx in range(X) if dz or dx]
    peers += [(me_p, j_of(zl + d, y, core)) for d in range(1, ZL)]
    peers += [(me_p, j_of(zl, y + d, core)) for d in (1, Y - 1)] + [(me_p, j_of(zl, y, 1 - core))]
    for p, j in peers:
        pl.semaphore_signal(barrier, inc=1, device_id=(p, j), device_id_type=MESH)

    lane = lax.broadcasted_iota(jnp.int32, (npc, nk * npv), 1) // npv

    @pl.loop(0, w_ref.shape[2] // 128)
    def _(a):
        at = pl.multiple_of(a * 128, 128)
        block = w_ref[0, :, pl.ds(at, 128)].astype(jnp.float32)
        block = jnp.concatenate([block, jnp.zeros((128 - own, 128), jnp.float32)], axis=0)
        wt[pl.ds(at, 128), :] = block.T.astype(jnp.bfloat16)

    acc[...] = jnp.zeros_like(acc)
    pl.semaphore_wait(barrier, len(peers))

    for dz in ORDER:
        for dx in range(X):
            to_x = lax.rem(x + dx, X)
            to = p_of(to_x, zh + ZH - dz)
            slot = dz * X + x
            if dz or dx:
                send(con_ref.at[:, to], con_in.at[slot], sent_sem.at[0], con_sem.at[dz], to, me_j)
            else:
                pltpu.make_async_copy(con_ref.at[:, to], con_in.at[slot], con_sem.at[dz]).start()

    @pl.loop(0, NJ)
    def _(j):
        jz, jy, jc = j // (Y * CORES), lax.rem(j // CORES, Y), lax.rem(j, CORES)
        at = pl.multiple_of((jc * ZL + jz) * 128, 128)
        from_row = pl.multiple_of(j * own, 32)
        main = wt[pl.ds(from_row, own), :]
        for i in range(X - 1):
            spare = wt[pl.ds(pl.multiple_of(from_row + 32 * i, 32), 32), :]
            right[jy * (X - 1) + i, pl.ds(at, own), 0:128] = main
            right[jy * (X - 1) + i, pl.ds(at + own, 32), 0:128] = jnp.zeros_like(spare)
            right[jy * (X - 1) + i, pl.ds(at, own), 128:256] = jnp.zeros_like(main)
            right[jy * (X - 1) + i, pl.ds(at + own, 32), 128:256] = spare

    for q in range(NP):
        value = jnp.zeros((npc, nk * npv), jnp.int32)
        for k in range(nk):
            value = jnp.where(lane == k, table_ref[k, q], value)
        label[q] = value

    def onward(n, z, sy, up, down):
        slot = slot_of(sy, core, z, n)
        chunk = wide.at[slot]
        for go, d in ((up, 1), (down, Y - 1)):
            if go is not None:

                @pl.when(go)
                def _():
                    send(chunk, chunk, sent_sem.at[1], hop_sem.at[slot], me_p, j_of(zl, y + d, core))

        send(chunk, chunk, sent_sem.at[2], pair_sem.at[lax.rem(sy, Y)], me_p, j_of(zl, y, 1 - core))

    for n, dz in SEQUENCE:
        slot = slot_of(y, core, zl + dz, n)
        if dz == 0:
            wait(con_in.at[pl.ds(n * X, X)], con_sem.at[n])
            parts = [con_in[n * X + i].astype(jnp.float32).reshape(rows, own) for i in range(X)]
            for i in range(X - 1):
                packed = jnp.concatenate([parts[i], parts[X - 1][:, 32 * i : 32 * i + 32]], axis=1)
                wide[slot, i * rows : (i + 1) * rows, :] = packed.astype(jnp.bfloat16)
            for d in range(1, ZL):
                send(wide.at[slot], wide.at[slot], sent_sem.at[1], hop_sem.at[slot], me_p, j_of(zl + d, y, core))
        else:
            wait(wide.at[slot], hop_sem.at[slot])
        onward(n, zl + dz, y, True, True)

    for dz in ORDER:
        for dx in range(X):
            to = p_of(lax.rem(x + dx, X), zh + ZH - dz)
            slot = dz * X + x
            if dz or dx:
                send(val_ref.at[:, to], val_in.at[slot], sent_sem.at[3], val_sem, to, me_j)
            else:
                pltpu.make_async_copy(val_ref.at[:, to], val_in.at[slot], val_sem).start()

    def multiply(sy, i):
        left = [
            wide[pl.ds(slot_of(sy, c, z, 0), ZH), i * rows : (i + 1) * rows, :].reshape(ZH * rows, 128)
            for c in range(CORES)
            for z in range(ZL)
        ]
        acc[i] += jnp.dot(
            jnp.concatenate(left, axis=1), right[lax.rem(sy, Y) * (X - 1) + i], preferred_element_type=jnp.float32
        )

    def pair_ready(sy):
        wait(wide.at[pl.ds(slot_of(sy, 1 - core, 0, 0), ZL * ZH)], pair_sem.at[lax.rem(sy, Y)])

    @pl.loop(1, Y // 2 + 1)
    def _(t):
        below, above = y + Y - t, y + t
        for at, (n, dz) in enumerate(SEQUENCE):
            for sy, reach, up in ((below, REACH_UP[n], True), (above, REACH_DOWN[n], False)):

                @pl.when(t <= reach)
                def _():
                    slot = slot_of(sy, core, zl + dz, n)
                    wait(wide.at[slot], hop_sem.at[slot])
                    go = t < reach
                    onward(n, zl + dz, sy, go if up else None, None if up else go)

            if at % 2:
                i = at // 4
                if at % 4 == 1:
                    if i == 0:
                        pair_ready(below + 1)
                    multiply(below + 1, i)
                else:

                    @pl.when(t > 1)
                    def _():
                        if i == 0:
                            pair_ready(above + Y - 1)
                        multiply(above + Y - 1, i)

    pair_ready(y + Y // 2)
    for i in range(X - 1):
        multiply(y + Y // 2, i)

    wait(val_in, val_sem)
    for n in ORDER:
        for i in range(X):
            slot = n * X + i
            here = slice(n * rows, (n + 1) * rows)
            if i < X - 1:
                u = acc[i, here, 0:own]
            else:
                u = acc[0, here, 128 : 128 + own] + acc[1, here, 128 : 128 + own] + acc[2, here, 128 : 128 + own]
            high = u.astype(jnp.bfloat16)
            low = (u - high.astype(jnp.float32)).astype(jnp.bfloat16)
            both = lax.dot_general(
                jnp.concatenate([high, low], axis=0), val_in[slot].reshape(nk * npv, own),
                (((1,), (1,)), ((), ())), preferred_element_type=jnp.float32,
            )
            both = both[:rows] + both[rows:]
            tile = jnp.zeros((npc, nk * npv), jnp.float32)
            for k in range(nk):
                tile = jnp.where(lane == k, both[k * npc : (k + 1) * npc], tile)
            part[slot] = tile
            to_p = p_of(i, zh + n)
            to_j = j_of(1, to_p // CORES, lax.rem(to_p, CORES))

            @pl.when(to_j == me_j)
            def _():
                pltpu.make_async_copy(part.at[slot], tiles.at[me_j], tile_sem).start()

            @pl.when(to_j != me_j)
            def _():
                send(part.at[slot], tiles.at[me_j], sent_sem.at[4], tile_sem, me_p, to_j)

    @pl.when(zl == 1)
    def _():
        wait(tiles, tile_sem)
        sums = [tiles[j] for j in range(NJ)]
        while len(sums) > 1:
            sums = [a + b for a, b in zip(sums[::2], sums[1::2])] + sums[len(sums) // 2 * 2 :]
        total[...] = sums[0]
        to_p = y * CORES + core

        @pl.loop(0, NJ)
        def _(j):
            itself = (to_p == me_p) & (j == me_j)

            @pl.when(itself)
            def _():
                pltpu.make_async_copy(total, back.at[me_p], back_sem).start()

            @pl.when(jnp.logical_not(itself))
            def _():
                send(total, back.at[me_p], sent_sem.at[5], back_sem, to_p, j)

    wait(back, back_sem)
    for j in range(NP):
        chosen = jnp.zeros((npc, nk * npv), jnp.float32)
        for q in range(NP):
            chosen = jnp.where(label[q] == j, back[q], chosen)
        for k in range(nk):
            out_ref[k, j] = chosen[:, k * npv : (k + 1) * npv]

    hops = sum(REACH_UP + REACH_DOWN) * ZL + (ZL - 1) * ZH
    wait(con_in.at[pl.ds(0, NP - 1)], sent_sem.at[0])
    wait(wide.at[pl.ds(0, hops)], sent_sem.at[1])
    wait(wide.at[pl.ds(0, NJ // CORES * ZH)], sent_sem.at[2])
    wait(val_in.at[pl.ds(0, NP - 1)], sent_sem.at[3])
    adds_up = zl == 1

    @pl.when(adds_up)
    def _():
        wait(part.at[pl.ds(0, NP - 1)], sent_sem.at[4])

        @pl.when(y * CORES + core == me_p)
        def _():
            wait(tiles.at[pl.ds(0, NJ - 1)], sent_sem.at[5])

        @pl.when(y * CORES + core != me_p)
        def _():
            wait(tiles, sent_sem.at[5])

    @pl.when(jnp.logical_not(adds_up))
    def _():
        wait(part, sent_sem.at[4])


def per_device(valence, conduction, screened, kq_table):
    nk, nq, npv, own = valence.shape
    npc = conduction.shape[2]
    rows = nk * npc
    in_place = pl.BlockSpec(memory_space=pl.ANY)
    return pl.pallas_call(
        kernel,
        out_shape=jax.ShapeDtypeStruct((nk, nq, npc, npv), jnp.float32),
        in_specs=[
            in_place,
            in_place,
            pl.BlockSpec(memory_space=pltpu.VMEM),
            pl.BlockSpec(memory_space=pltpu.SMEM),
        ],
        out_specs=pl.BlockSpec(memory_space=pltpu.VMEM),
        scratch_shapes=[
            pltpu.VMEM((NP, nk, npc, own), jnp.bfloat16),
            pltpu.VMEM((NP, nk, npv, own), jnp.bfloat16),
            pltpu.VMEM((NJ * ZH, (X - 1) * rows, 128), jnp.bfloat16),
            pltpu.VMEM((Y * (X - 1), CORES * ZL * 128, 256), jnp.bfloat16),
            pltpu.VMEM((NJ * own, 128), jnp.bfloat16),
            pltpu.VMEM((X - 1, ZH * rows, 256), jnp.float32),
            pltpu.VMEM((NP, npc, nk * npv), jnp.float32),
            pltpu.VMEM((NJ, npc, nk * npv), jnp.float32),
            pltpu.VMEM((npc, nk * npv), jnp.float32),
            pltpu.VMEM((NP, npc, nk * npv), jnp.float32),
            pltpu.VMEM((NP, npc, nk * npv), jnp.int32),
            pltpu.SemaphoreType.DMA((ZH,)),
            pltpu.SemaphoreType.DMA,
            pltpu.SemaphoreType.DMA((NJ * ZH,)),
            pltpu.SemaphoreType.DMA((Y,)),
            pltpu.SemaphoreType.DMA,
            pltpu.SemaphoreType.DMA,
            pltpu.SemaphoreType.DMA((6,)),
        ],
        compiler_params=pltpu.CompilerParams(
            collective_id=0, has_side_effects=True, vmem_limit_bytes=48 * 1024 * 1024
        ),
    )(valence, conduction, screened, kq_table)


def solution(mesh):
    return jax.shard_map(
        per_device,
        mesh=mesh,
        in_specs=(
            P("pb", None, None, "ga"),
            P("pb", None, None, "ga"),
            P("pb", "ga", None),
            P("pb", None),
        ),
        out_specs=P("pb", None, None, None),
        check_vma=False,
    )
```

```python
import jax
import jax.numpy as jnp
from jax import lax
from jax.experimental import pallas as pl
from jax.experimental.pallas import tpu as pltpu
from jax.sharding import PartitionSpec as P

MESH = pl.DeviceIdType.MESH
X, ZH, ZL, Y, CORES = 4, 4, 3, 8, 2
NP, NJ = X * ZH, ZL * Y * CORES
NS = ZL * Y
REACH_UP = (4, 3, 3, 4)
REACH_DOWN = (3, 4, 4, 3)
PREPARE = 6


def kernel(
    val_ref, con_ref, w_hbm, table_hbm, out_ref,
    con_in, val_in, val_pair, wide, w_ref, table_ref, wt, wt_pair, acc, part, tiles, total, back, label,
    entered, con_sem, val_sem, val_pair_sem, wt_pair_sem, hop_sem, tile_sem, back_sem, sent_sem, load_sem,
):
    me_p, me_j = lax.axis_index("pb"), lax.axis_index("ga")
    x, zh = me_p // ZH, lax.rem(me_p, ZH)
    zl, y, core = me_j // (Y * CORES), lax.rem(me_j // CORES, Y), lax.rem(me_j, CORES)
    nk, _, npc, own = con_ref.shape
    npv = val_ref.shape[2]
    rows = nk * npc
    spare = 128 - own

    def p_of(px, pz):
        return px * ZH + lax.rem(pz, ZH)

    def j_of(jz, jy, jc):
        return (lax.rem(jz, ZL) * Y + lax.rem(jy, Y)) * CORES + jc

    def slot_of(sy, sz, n):
        return (lax.rem(sy, Y) * ZL + lax.rem(sz, ZL)) * ZH + n

    def send(src, dst, sent, arrived, p, j):
        pltpu.make_async_remote_copy(
            src_ref=src, dst_ref=dst, send_sem=sent, recv_sem=arrived, device_id=(p, j), device_id_type=MESH
        ).start()

    def wait(ref, sem):
        pltpu.make_async_copy(ref, ref, sem).wait()

    pair = j_of(zl, y, 1 - core)
    load_w = pltpu.make_async_copy(w_hbm.at[0], w_ref, load_sem.at[0])
    load_table = pltpu.make_async_copy(table_hbm, table_ref, load_sem.at[1])
    load_w.start()
    load_table.start()

    barrier = pltpu.get_barrier_semaphore()
    near = [(p_of(lax.rem(x + d, X), zh), me_j) for d in range(1, X)]
    near += [(me_p, j_of(zl + d, y, core)) for d in range(1, ZL)]
    near += [(me_p, j_of(zl, y + d, core)) for d in (1, Y - 1)] + [(me_p, pair)]
    for p, j in near:
        pl.semaphore_signal(barrier, inc=1, device_id=(p, j), device_id_type=MESH)
    for d in range(1, ZH):

        @pl.when(zh + d < ZH)
        def _():
            for to_x in range(X):
                pl.semaphore_signal(barrier, inc=1, device_id=(p_of(to_x, zh + d), me_j), device_id_type=MESH)

    acc[...] = jnp.zeros_like(acc)
    pl.semaphore_wait(barrier, len(near) + X * zh)

    def exchange(ref, into, sent, sem, d):
        slot = (ZH - d) % ZH * X + x
        for dx in range(X):
            to = p_of(lax.rem(x + dx, X), zh + d)
            if d or dx:
                send(ref.at[:, to], into.at[slot], sent_sem.at[sent], sem.at[(ZH - d) % ZH], to, me_j)
            else:
                pltpu.make_async_copy(ref.at[:, to], into.at[slot], sem.at[0]).start()

    exchange(con_ref, con_in, 0, con_sem, 0)
    for d in range(1, ZH):

        @pl.when(zh + d >= ZH)
        def _():
            for to_x in range(X):
                pl.semaphore_signal(
                    entered.at[ZH - d], inc=1, device_id=(p_of(to_x, zh + d), me_j), device_id_type=MESH
                )

    for d in (1, 3, 2):

        @pl.when(zh + d >= ZH)
        def _():
            exchange(con_ref, con_in, 0, con_sem, d)

    exchange(val_ref, val_in, 3, val_sem, 0)

    def upward():
        for d in range(1, ZH):

            @pl.when(zh + d < ZH)
            def _():
                pl.semaphore_wait(entered.at[d], X)
                exchange(con_ref, con_in, 0, con_sem, d)

    def valence_out():
        for d in (1, 3, 2):
            exchange(val_ref, val_in, 3, val_sem, d)

    def prepare(piece):
        if piece == 0:
            load_w.wait()
        tiles_each = w_ref.shape[1] // 128 // PREPARE

        @pl.loop(piece * tiles_each, (piece + 1) * tiles_each)
        def _(a):
            at = pl.multiple_of(a * 128, 128)
            block = w_ref[:, pl.ds(at, 128)].astype(jnp.float32)
            block = jnp.concatenate([block, jnp.zeros((spare, 128), jnp.float32)], axis=0).T.astype(jnp.bfloat16)
            for b in range(128 // 32):
                row = a * (128 // 32) + b
                wt[row // (own // 32), pl.ds(pl.multiple_of(lax.rem(row, own // 32) * 32, 32), 32), :] = block[32 * b : 32 * b + 32]

    def screened_out():
        by_core = wt.reshape(NS, CORES, own, 128)
        send(by_core.at[:, 1 - core], wt_pair, sent_sem.at[6], wt_pair_sem, me_p, pair)

    def labels():
        load_table.wait()
        lane = lax.broadcasted_iota(jnp.int32, (npc, nk * npv), 1) // npv
        for q in range(NP):
            value = jnp.zeros((npc, nk * npv), jnp.int32)
            for k in range(nk):
                value = jnp.where(lane == k, table_ref[k, q], value)
            label[q] = value

    def onward(slot, up, down):
        for go, d in ((up, 1), (down, Y - 1)):
            if go:
                send(wide.at[slot], wide.at[slot], sent_sem.at[1], hop_sem.at[slot], me_p, j_of(zl, y + d, core))

    def begin(n):
        slot = slot_of(y, zl, n)
        wait(con_in.at[pl.ds(n * X, X)], con_sem.at[n])
        parts = [con_in[n * X + i].astype(jnp.float32).reshape(rows, own) for i in range(X)]
        for i in range(X - 1):
            packed = jnp.concatenate([parts[i], parts[X - 1][:, spare * i : spare * (i + 1)]], axis=1)
            wide[slot, i * rows : (i + 1) * rows, :] = packed.astype(jnp.bfloat16)
        for d in range(1, ZL):
            send(wide.at[slot], wide.at[slot], sent_sem.at[1], hop_sem.at[slot], me_p, j_of(zl + d, y, core))
        onward(slot, True, True)

    def hop(n, t):
        for dz in range(ZL):
            if t == 0 and dz:
                slot = slot_of(y, zl + dz, n)
                wait(wide.at[slot], hop_sem.at[slot])
                onward(slot, True, True)
            if t:
                for sy, reach, up in ((y + Y - t, REACH_UP[n], True), (y + t, REACH_DOWN[n], False)):
                    if t <= reach:
                        slot = slot_of(sy, zl + dz, n)
                        wait(wide.at[slot], hop_sem.at[slot])
                        onward(slot, up and t < reach, not up and t < reach)

    def multiply(n, t):
        for sy in [y + t] if t in (0, Y // 2) else [y + Y - t, y + t]:
            left, right = [], []
            for z in range(ZL):
                chunk = wide[slot_of(sy, z, n)]
                thirds = [chunk[i * rows : (i + 1) * rows].astype(jnp.float32) for i in range(X - 1)]
                fourth = jnp.concatenate([third[:, own:] for third in thirds] + [thirds[0][:, own:]], axis=1)
                left.append(jnp.concatenate([chunk, fourth.astype(jnp.bfloat16)], axis=0))
                source = z * Y + lax.rem(sy, Y)
                both = jnp.concatenate([wt[source * CORES + core], wt_pair[source]], axis=1)
                right += [both, jnp.zeros((spare, 256), jnp.bfloat16)]
            product = jnp.dot(
                jnp.concatenate(left, axis=1), jnp.concatenate(right, axis=0), preferred_element_type=jnp.float32
            )
            acc[...] = product if t == 0 else acc[...] + product

    def valence_pair(n):
        here = pl.ds(n * X, X)
        wait(val_in.at[here], val_sem.at[n])
        send(val_in.at[here], val_pair.at[here], sent_sem.at[2], val_pair_sem.at[n], me_p, pair)

    def second(n):
        wait(val_pair.at[pl.ds(n * X, X)], val_pair_sem.at[n])
        lane = lax.broadcasted_iota(jnp.int32, (npc, nk * npv), 1) // npv
        for i in range(X):
            u = acc[i * rows : (i + 1) * rows, :]
            high = u.astype(jnp.bfloat16)
            low = (u - high.astype(jnp.float32)).astype(jnp.bfloat16)
            stacked = jnp.concatenate([high, low], axis=0)
            both = sum(
                lax.dot_general(
                    stacked[:, at : at + own], from_[n * X + i].reshape(nk * npv, own),
                    (((1,), (1,)), ((), ())), preferred_element_type=jnp.float32,
                )
                for at, from_ in ((0, val_in), (128, val_pair))
            )
            both = both[:rows] + both[rows:]
            tile = jnp.zeros((npc, nk * npv), jnp.float32)
            for k in range(nk):
                tile = jnp.where(lane == k, both[k * npc : (k + 1) * npc], tile)
            part[n * X + i] = tile
        for i in range(X):
            to_p = p_of(i, zh + n)
            to_j = j_of(1, to_p // CORES, lax.rem(to_p, CORES))

            @pl.when(to_j == me_j)
            def _():
                pltpu.make_async_copy(part.at[n * X + i], tiles.at[me_j], tile_sem).start()

            @pl.when(to_j != me_j)
            def _():
                send(part.at[n * X + i], tiles.at[me_j], sent_sem.at[4], tile_sem, me_p, to_j)

    adds_for = y * CORES + core

    def add_up(n):
        @pl.when((zl == 1) & (lax.rem(adds_for + ZH - zh, ZH) == n))
        def _():
            wait(tiles, tile_sem)
            sums = [tiles[j] for j in range(NJ)]
            while len(sums) > 1:
                sums = [a + b for a, b in zip(sums[::2], sums[1::2])] + sums[len(sums) // 2 * 2 :]
            total[...] = sums[0]

            @pl.loop(0, NJ)
            def _(j):
                itself = (adds_for == me_p) & (j == me_j)

                @pl.when(itself)
                def _():
                    pltpu.make_async_copy(total, back.at[me_p], back_sem).start()

                @pl.when(jnp.logical_not(itself))
                def _():
                    send(total, back.at[me_p], sent_sem.at[5], back_sem, adds_for, j)

    def screened_ready():
        wait(wt_pair, wt_pair_sem)

    for step in (
        (begin, 0), (prepare, 0), (prepare, 1), (hop, 0, 0), (upward,), (prepare, 2), (prepare, 3), (hop, 0, 1),
        (prepare, 4), (prepare, 5), (screened_out,), (valence_out,), (begin, 1), (hop, 0, 2), (labels,), (hop, 1, 0),
        (hop, 0, 3), (valence_pair, 0), (screened_ready,), (multiply, 0, 0), (hop, 1, 1), (multiply, 0, 1), (hop, 0, 4),
        (multiply, 0, 2), (hop, 1, 2), (multiply, 0, 3), (multiply, 0, 4), (begin, 3), (second, 0), (hop, 3, 0),
        (multiply, 1, 0), (hop, 1, 3), (multiply, 1, 1), (valence_pair, 1), (hop, 3, 1), (multiply, 1, 2), (hop, 1, 4),
        (multiply, 1, 3), (hop, 3, 2), (multiply, 1, 4), (begin, 2), (second, 1), (add_up, 0), (hop, 2, 0),
        (multiply, 3, 0), (hop, 3, 3), (multiply, 3, 1), (valence_pair, 3), (hop, 2, 1), (multiply, 3, 2), (hop, 3, 4),
        (multiply, 3, 3), (multiply, 3, 4), (hop, 2, 2), (second, 3), (multiply, 2, 0), (add_up, 1), (hop, 2, 3),
        (multiply, 2, 1), (multiply, 2, 2), (valence_pair, 2), (add_up, 3), (hop, 2, 4), (multiply, 2, 3),
        (multiply, 2, 4), (second, 2), (add_up, 2),
    ):
        step[0](*step[1:])

    wait(back, back_sem)
    for j in range(NP):
        chosen = jnp.zeros((npc, nk * npv), jnp.float32)
        for q in range(NP):
            chosen = jnp.where(label[q] == j, back[q], chosen)
        for k in range(nk):
            out_ref[k, j] = chosen[:, k * npv : (k + 1) * npv]

    hops = sum(REACH_UP + REACH_DOWN) * ZL + (ZL - 1) * ZH
    wait(con_in.at[pl.ds(0, NP - 1)], sent_sem.at[0])
    wait(wide.at[pl.ds(0, hops)], sent_sem.at[1])
    wait(val_in, sent_sem.at[2])
    wait(val_in.at[pl.ds(0, NP - 1)], sent_sem.at[3])
    wait(wt_pair, sent_sem.at[6])

    @pl.when(zl == 1)
    def _():
        wait(part.at[pl.ds(0, NP - 1)], sent_sem.at[4])

        @pl.when(adds_for == me_p)
        def _():
            wait(tiles.at[pl.ds(0, NJ - 1)], sent_sem.at[5])

        @pl.when(adds_for != me_p)
        def _():
            wait(tiles, sent_sem.at[5])

    @pl.when(zl != 1)
    def _():
        wait(part, sent_sem.at[4])


def per_device(valence, conduction, screened, kq_table):
    nk, nq, npv, own = valence.shape
    npc = conduction.shape[2]
    rows = nk * npc
    return pl.pallas_call(
        kernel,
        out_shape=jax.ShapeDtypeStruct((nk, nq, npc, npv), jnp.float32),
        in_specs=[pl.BlockSpec(memory_space=pltpu.HBM)] * 4,
        out_specs=pl.BlockSpec(memory_space=pltpu.VMEM),
        scratch_shapes=[
            pltpu.VMEM((NP, nk, npc, own), jnp.bfloat16),
            pltpu.VMEM((NP, nk, npv, own), jnp.bfloat16),
            pltpu.VMEM((NP, nk, npv, own), jnp.bfloat16),
            pltpu.VMEM((NS * ZH, (X - 1) * rows, 128), jnp.bfloat16),
            pltpu.VMEM((own, NJ * own), jnp.bfloat16),
            pltpu.SMEM((nk, nq), jnp.int32),
            pltpu.VMEM((NJ, own, 128), jnp.bfloat16),
            pltpu.VMEM((NS, own, 128), jnp.bfloat16),
            pltpu.VMEM((X * rows, 256), jnp.float32),
            pltpu.VMEM((NP, npc, nk * npv), jnp.float32),
            pltpu.VMEM((NJ, npc, nk * npv), jnp.float32),
            pltpu.VMEM((npc, nk * npv), jnp.float32),
            pltpu.VMEM((NP, npc, nk * npv), jnp.float32),
            pltpu.VMEM((NP, npc, nk * npv), jnp.int32),
            pltpu.SemaphoreType.REGULAR((ZH,)),
            pltpu.SemaphoreType.DMA((ZH,)),
            pltpu.SemaphoreType.DMA((ZH,)),
            pltpu.SemaphoreType.DMA((ZH,)),
            pltpu.SemaphoreType.DMA,
            pltpu.SemaphoreType.DMA((NS * ZH,)),
            pltpu.SemaphoreType.DMA,
            pltpu.SemaphoreType.DMA,
            pltpu.SemaphoreType.DMA((7,)),
            pltpu.SemaphoreType.DMA((2,)),
        ],
        compiler_params=pltpu.CompilerParams(collective_id=0, has_side_effects=True, vmem_limit_bytes=67043328),
    )(valence, conduction, screened, kq_table)


def solution(mesh):
    return jax.shard_map(
        per_device,
        mesh=mesh,
        in_specs=(
            P("pb", None, None, "ga"),
            P("pb", None, None, "ga"),
            P("pb", "ga", None),
            P("pb", None),
        ),
        out_specs=P("pb", None, None, None),
        check_vma=False,
    )
```

```python
import jax
import jax.numpy as jnp
from jax import lax
from jax.experimental import pallas as pl
from jax.experimental.pallas import tpu as pltpu
from jax.sharding import PartitionSpec as P

MESH = pl.DeviceIdType.MESH
X, ZH, ZL, Y, CORES = 4, 4, 3, 8, 2
NP, NJ = X * ZH, ZL * Y * CORES
NS = ZL * Y
REACH_UP = (4, 3, 3, 4)
REACH_DOWN = (3, 4, 4, 3)
PREPARE = 6


def kernel(
    val_ref, con_ref, w_hbm, table_hbm, out_ref,
    con_in, val_in, val_pair, wide, w_ref, table_ref, wt, wt_pair, acc, part, tiles, total, back, label,
    con_sem, val_sem, val_pair_sem, wt_pair_sem, hop_sem, tile_sem, back_sem, sent_sem, load_sem,
):
    me_p, me_j = lax.axis_index("pb"), lax.axis_index("ga")
    x, zh = me_p // ZH, lax.rem(me_p, ZH)
    zl, y, core = me_j // (Y * CORES), lax.rem(me_j // CORES, Y), lax.rem(me_j, CORES)
    nk, _, npc, own = con_ref.shape
    npv = val_ref.shape[2]
    rows = nk * npc
    spare = 128 - own

    def p_of(px, pz):
        return px * ZH + lax.rem(pz, ZH)

    def j_of(jz, jy, jc):
        return (lax.rem(jz, ZL) * Y + lax.rem(jy, Y)) * CORES + jc

    def slot_of(sy, sz, n):
        return (lax.rem(sy, Y) * ZL + lax.rem(sz, ZL)) * ZH + n

    def send(src, dst, sent, arrived, p, j):
        pltpu.make_async_remote_copy(
            src_ref=src, dst_ref=dst, send_sem=sent, recv_sem=arrived, device_id=(p, j), device_id_type=MESH
        ).start()

    def wait(ref, sem):
        pltpu.make_async_copy(ref, ref, sem).wait()

    pair = j_of(zl, y, 1 - core)
    load_w = pltpu.make_async_copy(w_hbm.at[0], w_ref, load_sem.at[0])
    load_table = pltpu.make_async_copy(table_hbm, table_ref, load_sem.at[1])
    load_w.start()
    load_table.start()

    barrier = pltpu.get_barrier_semaphore()
    near = [(p_of(lax.rem(x + dx, X), zh + d), me_j) for d in range(ZH) for dx in range(X) if d or dx]
    near += [(me_p, j_of(zl + d, y, core)) for d in range(1, ZL)]
    near += [(me_p, j_of(zl, y + d, core)) for d in (1, Y - 1)] + [(me_p, pair)]
    for p, j in near:
        pl.semaphore_signal(barrier, inc=1, device_id=(p, j), device_id_type=MESH)
    pl.semaphore_wait(barrier, len(near))

    def exchange(ref, into, sent, sem, d):
        slot = (ZH - d) % ZH * X + x
        for dx in range(X):
            to = p_of(lax.rem(x + dx, X), zh + d)
            if d or dx:
                send(ref.at[:, to], into.at[slot], sent_sem.at[sent], sem.at[(ZH - d) % ZH], to, me_j)
            else:
                pltpu.make_async_copy(ref.at[:, to], into.at[slot], sem.at[0]).start()

    for d in (0, 1, 3, 2):
        exchange(con_ref, con_in, 0, con_sem, d)

    def valence_out():
        for d in (0, 1, 3, 2):
            exchange(val_ref, val_in, 3, val_sem, d)

    def prepare(piece):
        if piece == 0:
            load_w.wait()
        tiles_each = w_ref.shape[1] // 128 // PREPARE

        @pl.loop(piece * tiles_each, (piece + 1) * tiles_each)
        def _(a):
            at = pl.multiple_of(a * 128, 128)
            block = w_ref[:, pl.ds(at, 128)].astype(jnp.float32)
            block = jnp.concatenate([block, jnp.zeros((spare, 128), jnp.float32)], axis=0).T.astype(jnp.bfloat16)
            for b in range(128 // 32):
                row = a * (128 // 32) + b
                wt[row // (own // 32), pl.ds(pl.multiple_of(lax.rem(row, own // 32) * 32, 32), 32), :] = block[32 * b : 32 * b + 32]

    def screened_out():
        by_core = wt.reshape(NS, CORES, own, 128)
        send(by_core.at[:, 1 - core], wt_pair, sent_sem.at[6], wt_pair_sem, me_p, pair)

    def labels():
        load_table.wait()
        lane = lax.broadcasted_iota(jnp.int32, (npc, nk * npv), 1) // npv
        for q in range(NP):
            value = jnp.zeros((npc, nk * npv), jnp.int32)
            for k in range(nk):
                value = jnp.where(lane == k, table_ref[k, q], value)
            label[q] = value

    def onward(slot, up, down):
        for go, d in ((up, 1), (down, Y - 1)):
            if go:
                send(wide.at[slot], wide.at[slot], sent_sem.at[1], hop_sem.at[slot], me_p, j_of(zl, y + d, core))

    def begin(n):
        slot = slot_of(y, zl, n)
        wait(con_in.at[pl.ds(n * X, X)], con_sem.at[n])
        parts = [con_in[n * X + i].astype(jnp.float32).reshape(rows, own) for i in range(X)]
        for i in range(X - 1):
            packed = jnp.concatenate([parts[i], parts[X - 1][:, spare * i : spare * (i + 1)]], axis=1)
            wide[slot, i * rows : (i + 1) * rows, :] = packed.astype(jnp.bfloat16)
        for d in range(1, ZL):
            send(wide.at[slot], wide.at[slot], sent_sem.at[1], hop_sem.at[slot], me_p, j_of(zl + d, y, core))
        onward(slot, True, True)

    def hop(n, t):
        for dz in range(ZL):
            if t == 0 and dz:
                slot = slot_of(y, zl + dz, n)
                wait(wide.at[slot], hop_sem.at[slot])
                onward(slot, True, True)
            if t:
                for sy, reach, up in ((y + Y - t, REACH_UP[n], True), (y + t, REACH_DOWN[n], False)):
                    if t <= reach:
                        slot = slot_of(sy, zl + dz, n)
                        wait(wide.at[slot], hop_sem.at[slot])
                        onward(slot, up and t < reach, not up and t < reach)

    def multiply(n, t):
        for sy in [y + t] if t in (0, Y // 2) else [y + Y - t, y + t]:
            left, right = [], []
            for z in range(ZL):
                chunk = wide[slot_of(sy, z, n)]
                thirds = [chunk[i * rows : (i + 1) * rows].astype(jnp.float32) for i in range(X - 1)]
                fourth = jnp.concatenate([third[:, own:] for third in thirds] + [thirds[0][:, own:]], axis=1)
                left.append(jnp.concatenate([chunk, fourth.astype(jnp.bfloat16)], axis=0))
                source = z * Y + lax.rem(sy, Y)
                both = jnp.concatenate([wt[source * CORES + core], wt_pair[source]], axis=1)
                right += [both, jnp.zeros((spare, 256), jnp.bfloat16)]
            product = jnp.dot(
                jnp.concatenate(left, axis=1), jnp.concatenate(right, axis=0), preferred_element_type=jnp.float32
            )
            acc[n] = product if t == 0 else acc[n] + product

    def valence_pair(n):
        here = pl.ds(n * X, X)
        wait(val_in.at[here], val_sem.at[n])
        send(val_in.at[here], val_pair.at[here], sent_sem.at[2], val_pair_sem.at[n], me_p, pair)

    def second(n):
        wait(val_pair.at[pl.ds(n * X, X)], val_pair_sem.at[n])
        lane = lax.broadcasted_iota(jnp.int32, (npc, nk * npv), 1) // npv
        for i in range(X):
            u = acc[n, i * rows : (i + 1) * rows, :]
            high = u.astype(jnp.bfloat16)
            low = (u - high.astype(jnp.float32)).astype(jnp.bfloat16)
            stacked = jnp.concatenate([high, low], axis=0)
            both = sum(
                lax.dot_general(
                    stacked[:, at : at + own], from_[n * X + i].reshape(nk * npv, own),
                    (((1,), (1,)), ((), ())), preferred_element_type=jnp.float32,
                )
                for at, from_ in ((0, val_in), (128, val_pair))
            )
            both = both[:rows] + both[rows:]
            tile = jnp.zeros((npc, nk * npv), jnp.float32)
            for k in range(nk):
                tile = jnp.where(lane == k, both[k * npc : (k + 1) * npc], tile)
            part[n * X + i] = tile
        for i in range(X):
            to_p = p_of(i, zh + n)
            to_j = j_of(1, to_p // CORES, lax.rem(to_p, CORES))

            @pl.when(to_j == me_j)
            def _():
                pltpu.make_async_copy(part.at[n * X + i], tiles.at[me_j], tile_sem).start()

            @pl.when(to_j != me_j)
            def _():
                send(part.at[n * X + i], tiles.at[me_j], sent_sem.at[4], tile_sem, me_p, to_j)

    adds_for = y * CORES + core

    def add_up(n):
        @pl.when((zl == 1) & (lax.rem(adds_for + ZH - zh, ZH) == n))
        def _():
            wait(tiles, tile_sem)
            sums = [tiles[j] for j in range(NJ)]
            while len(sums) > 1:
                sums = [a + b for a, b in zip(sums[::2], sums[1::2])] + sums[len(sums) // 2 * 2 :]
            total[...] = sums[0]

            @pl.loop(0, NJ)
            def _(j):
                itself = (adds_for == me_p) & (j == me_j)

                @pl.when(itself)
                def _():
                    pltpu.make_async_copy(total, back.at[me_p], back_sem).start()

                @pl.when(jnp.logical_not(itself))
                def _():
                    send(total, back.at[me_p], sent_sem.at[5], back_sem, adds_for, j)

    def screened_ready():
        wait(wt_pair, wt_pair_sem)

    for step in (
        (begin, 0), (prepare, 0), (begin, 1), (prepare, 1), (hop, 0, 0), (begin, 3), (prepare, 2), (hop, 1, 0), (begin, 2),
        (prepare, 3), (hop, 3, 0), (prepare, 4), (hop, 2, 0), (valence_out,), (prepare, 5), (screened_out,), (labels,),
        (hop, 0, 1), (hop, 1, 1), (hop, 3, 1), (hop, 2, 1), (screened_ready,),
        (hop, 0, 2), (multiply, 0, 0), (multiply, 1, 0), (hop, 1, 2), (multiply, 3, 0), (multiply, 2, 0), (hop, 3, 2),
        (multiply, 0, 1), (hop, 2, 2), (multiply, 1, 1), (hop, 0, 3), (multiply, 3, 1), (multiply, 2, 1), (hop, 1, 3),
        (multiply, 0, 2), (multiply, 1, 2), (hop, 3, 3), (multiply, 3, 2), (hop, 2, 3), (multiply, 2, 2), (valence_pair, 0),
        (valence_pair, 1), (valence_pair, 3), (valence_pair, 2), (hop, 0, 4),
        (multiply, 0, 3), (multiply, 0, 4), (hop, 1, 4), (multiply, 1, 3), (multiply, 1, 4), (second, 0),
        (hop, 3, 4), (multiply, 3, 3), (multiply, 3, 4), (second, 1), (hop, 2, 4), (multiply, 2, 3), (multiply, 2, 4),
        (second, 3), (second, 2), (add_up, 0), (add_up, 1), (add_up, 3), (add_up, 2),
    ):
        step[0](*step[1:])

    wait(back, back_sem)
    for j in range(NP):
        chosen = jnp.zeros((npc, nk * npv), jnp.float32)
        for q in range(NP):
            chosen = jnp.where(label[q] == j, back[q], chosen)
        for k in range(nk):
            out_ref[k, j] = chosen[:, k * npv : (k + 1) * npv]

    hops = sum(REACH_UP + REACH_DOWN) * ZL + (ZL - 1) * ZH
    wait(con_in.at[pl.ds(0, NP - 1)], sent_sem.at[0])
    wait(wide.at[pl.ds(0, hops)], sent_sem.at[1])
    wait(val_in, sent_sem.at[2])
    wait(val_in.at[pl.ds(0, NP - 1)], sent_sem.at[3])
    wait(wt_pair, sent_sem.at[6])

    @pl.when(zl == 1)
    def _():
        wait(part.at[pl.ds(0, NP - 1)], sent_sem.at[4])

        @pl.when(adds_for == me_p)
        def _():
            wait(tiles.at[pl.ds(0, NJ - 1)], sent_sem.at[5])

        @pl.when(adds_for != me_p)
        def _():
            wait(tiles, sent_sem.at[5])

    @pl.when(zl != 1)
    def _():
        wait(part, sent_sem.at[4])


def per_device(valence, conduction, screened, kq_table):
    nk, nq, npv, own = valence.shape
    npc = conduction.shape[2]
    rows = nk * npc
    return pl.pallas_call(
        kernel,
        out_shape=jax.ShapeDtypeStruct((nk, nq, npc, npv), jnp.float32),
        in_specs=[pl.BlockSpec(memory_space=pltpu.HBM)] * 4,
        out_specs=pl.BlockSpec(memory_space=pltpu.VMEM),
        scratch_shapes=[
            pltpu.VMEM((NP, nk, npc, own), jnp.bfloat16),
            pltpu.VMEM((NP, nk, npv, own), jnp.bfloat16),
            pltpu.VMEM((NP, nk, npv, own), jnp.bfloat16),
            pltpu.VMEM((NS * ZH, (X - 1) * rows, 128), jnp.bfloat16),
            pltpu.VMEM((own, NJ * own), jnp.bfloat16),
            pltpu.SMEM((nk, nq), jnp.int32),
            pltpu.VMEM((NJ, own, 128), jnp.bfloat16),
            pltpu.VMEM((NS, own, 128), jnp.bfloat16),
            pltpu.VMEM((ZH, X * rows, 256), jnp.float32),
            pltpu.VMEM((NP, npc, nk * npv), jnp.float32),
            pltpu.VMEM((NJ, npc, nk * npv), jnp.float32),
            pltpu.VMEM((npc, nk * npv), jnp.float32),
            pltpu.VMEM((NP, npc, nk * npv), jnp.float32),
            pltpu.VMEM((NP, npc, nk * npv), jnp.int32),
            pltpu.SemaphoreType.DMA((ZH,)),
            pltpu.SemaphoreType.DMA((ZH,)),
            pltpu.SemaphoreType.DMA((ZH,)),
            pltpu.SemaphoreType.DMA,
            pltpu.SemaphoreType.DMA((NS * ZH,)),
            pltpu.SemaphoreType.DMA,
            pltpu.SemaphoreType.DMA,
            pltpu.SemaphoreType.DMA((7,)),
            pltpu.SemaphoreType.DMA((2,)),
        ],
        compiler_params=pltpu.CompilerParams(collective_id=0, has_side_effects=True, vmem_limit_bytes=67043328),
    )(valence, conduction, screened, kq_table)


def solution(mesh):
    return jax.shard_map(
        per_device,
        mesh=mesh,
        in_specs=(
            P("pb", None, None, "ga"),
            P("pb", None, None, "ga"),
            P("pb", "ga", None),
            P("pb", None),
        ),
        out_specs=P("pb", None, None, None),
        check_vma=False,
    )
```

```python
import jax
import jax.numpy as jnp
from jax import lax
from jax.experimental import pallas as pl
from jax.experimental.pallas import tpu as pltpu
from jax.sharding import PartitionSpec as P

MESH = pl.DeviceIdType.MESH
X, ZH, ZL, Y, CORES = 4, 4, 3, 8, 2
NP, NJ = X * ZH, ZL * Y * CORES
NS = ZL * Y
REACH_UP = (4, 3, 3, 4)
REACH_DOWN = (3, 4, 4, 3)
PREPARE = 6


def kernel(
    val_ref, con_ref, w_hbm, table_hbm, out_ref,
    con_in, val_in, val_pair, wide, w_ref, table_ref, wt, wt_pair, acc, part, tiles, total, back, label,
    con_sem, val_sem, val_pair_sem, wt_pair_sem, hop_sem, tile_sem, back_sem, sent_sem, load_sem,
):
    me_p, me_j = lax.axis_index("pb"), lax.axis_index("ga")
    x, zh = me_p // ZH, lax.rem(me_p, ZH)
    zl, y, core = me_j // (Y * CORES), lax.rem(me_j // CORES, Y), lax.rem(me_j, CORES)
    nk, _, npc, own = con_ref.shape
    npv = val_ref.shape[2]
    rows = nk * npc
    spare = 128 - own

    def p_of(px, pz):
        return px * ZH + lax.rem(pz, ZH)

    def j_of(jz, jy, jc):
        return (lax.rem(jz, ZL) * Y + lax.rem(jy, Y)) * CORES + jc

    def slot_of(sy, sz, n):
        return (lax.rem(sy, Y) * ZL + lax.rem(sz, ZL)) * ZH + n

    def send(src, dst, sent, arrived, p, j):
        pltpu.make_async_remote_copy(
            src_ref=src, dst_ref=dst, send_sem=sent, recv_sem=arrived, device_id=(p, j), device_id_type=MESH
        ).start()

    def wait(ref, sem):
        pltpu.make_async_copy(ref, ref, sem).wait()

    pair = j_of(zl, y, 1 - core)
    load_w = pltpu.make_async_copy(w_hbm.at[0], w_ref, load_sem.at[0])
    load_table = pltpu.make_async_copy(table_hbm, table_ref, load_sem.at[1])
    load_w.start()
    load_table.start()

    barrier = pltpu.get_barrier_semaphore()
    near = [(p_of(lax.rem(x + dx, X), zh + d), me_j) for d in range(ZH) for dx in range(X) if d or dx]
    near += [(me_p, j_of(zl + d, y, core)) for d in range(1, ZL)]
    near += [(me_p, j_of(zl, y + d, core)) for d in (1, Y - 1)] + [(me_p, pair)]
    for p, j in near:
        pl.semaphore_signal(barrier, inc=1, device_id=(p, j), device_id_type=MESH)
    pl.semaphore_wait(barrier, len(near))

    def exchange(ref, into, sent, sem, d):
        slot = (ZH - d) % ZH * X + x
        for dx in range(X):
            to = p_of(lax.rem(x + dx, X), zh + d)
            if d or dx:
                send(ref.at[:, to], into.at[slot], sent_sem.at[sent], sem.at[(ZH - d) % ZH], to, me_j)
            else:
                pltpu.make_async_copy(ref.at[:, to], into.at[slot], sem.at[0]).start()

    for d in (0, 1, 3, 2):
        exchange(con_ref, con_in, 0, con_sem, d)

    def valence_out():
        for d in (0, 1, 3, 2):
            exchange(val_ref, val_in, 3, val_sem, d)

    def prepare(piece):
        if piece == 0:
            load_w.wait()
        tiles_each = w_ref.shape[1] // 128 // PREPARE

        @pl.loop(piece * tiles_each, (piece + 1) * tiles_each)
        def _(a):
            at = pl.multiple_of(a * 128, 128)
            block = w_ref[:, pl.ds(at, 128)].astype(jnp.float32)
            block = jnp.concatenate([block, jnp.zeros((spare, 128), jnp.float32)], axis=0).T.astype(jnp.bfloat16)
            for b in range(128 // 32):
                row = a * (128 // 32) + b
                wt[row // (own // 32), pl.ds(pl.multiple_of(lax.rem(row, own // 32) * 32, 32), 32), :] = block[32 * b : 32 * b + 32]

    def screened_out():
        by_core = wt.reshape(NS, CORES, own, 128)
        send(by_core.at[:, 1 - core], wt_pair, sent_sem.at[6], wt_pair_sem, me_p, pair)

    def labels():
        load_table.wait()
        lane = lax.broadcasted_iota(jnp.int32, (npc, nk * npv), 1) // npv
        for q in range(NP):
            value = jnp.zeros((npc, nk * npv), jnp.int32)
            for k in range(nk):
                value = jnp.where(lane == k, table_ref[k, q], value)
            label[q] = value

    def onward(slot, up, down):
        for go, d in ((up, 1), (down, Y - 1)):
            if go:
                send(wide.at[slot], wide.at[slot], sent_sem.at[1], hop_sem.at[slot], me_p, j_of(zl, y + d, core))

    def begin(n):
        slot = slot_of(y, zl, n)
        wait(con_in.at[pl.ds(n * X, X)], con_sem.at[n])
        parts = [con_in[n * X + i].astype(jnp.float32).reshape(rows, own) for i in range(X)]
        for i in range(X - 1):
            packed = jnp.concatenate([parts[i], parts[X - 1][:, spare * i : spare * (i + 1)]], axis=1)
            wide[slot, i * rows : (i + 1) * rows, :] = packed.astype(jnp.bfloat16)
        for d in range(1, ZL):
            send(wide.at[slot], wide.at[slot], sent_sem.at[1], hop_sem.at[slot], me_p, j_of(zl + d, y, core))
        onward(slot, True, True)

    def enter(n):
        for dz in range(1, ZL):
            slot = slot_of(y, zl + dz, n)
            wait(wide.at[slot], hop_sem.at[slot])
            onward(slot, True, True)

    def offset(row):
        return lax.rem(row + ZH - zh, ZH)

    def hop(row, t):
        for dz in range(ZL):
            for sy, reach, up in ((y + Y - t, REACH_UP[row], True), (y + t, REACH_DOWN[row], False)):
                if t <= reach:
                    slot = slot_of(sy, zl + dz, offset(row))
                    wait(wide.at[slot], hop_sem.at[slot])
                    onward(slot, up and t < reach, not up and t < reach)

    def multiply(row, t):
        n = offset(row)
        for sy in [y + t] if t in (0, Y // 2) else [y + Y - t, y + t]:
            left, right = [], []
            for z in range(ZL):
                chunk = wide[slot_of(sy, z, n)]
                thirds = [chunk[i * rows : (i + 1) * rows].astype(jnp.float32) for i in range(X - 1)]
                fourth = jnp.concatenate([third[:, own:] for third in thirds] + [thirds[0][:, own:]], axis=1)
                left.append(jnp.concatenate([chunk, fourth.astype(jnp.bfloat16)], axis=0))
                source = z * Y + lax.rem(sy, Y)
                both = jnp.concatenate([wt[source * CORES + core], wt_pair[source]], axis=1)
                right += [both, jnp.zeros((spare, 256), jnp.bfloat16)]
            product = jnp.dot(
                jnp.concatenate(left, axis=1), jnp.concatenate(right, axis=0), preferred_element_type=jnp.float32
            )
            acc[n] = product if t == 0 else acc[n] + product

    def valence_pair(row):
        n = offset(row)
        here = pl.ds(n * X, X)
        wait(val_in.at[here], val_sem.at[n])
        send(val_in.at[here], val_pair.at[here], sent_sem.at[2], val_pair_sem.at[n], me_p, pair)

    def second(row):
        n = offset(row)
        wait(val_pair.at[pl.ds(n * X, X)], val_pair_sem.at[n])
        lane = lax.broadcasted_iota(jnp.int32, (npc, nk * npv), 1) // npv
        for i in range(X):
            u = acc[n, i * rows : (i + 1) * rows, :]
            high = u.astype(jnp.bfloat16)
            low = (u - high.astype(jnp.float32)).astype(jnp.bfloat16)
            stacked = jnp.concatenate([high, low], axis=0)
            both = sum(
                lax.dot_general(
                    stacked[:, at : at + own], from_[n * X + i].reshape(nk * npv, own),
                    (((1,), (1,)), ((), ())), preferred_element_type=jnp.float32,
                )
                for at, from_ in ((0, val_in), (128, val_pair))
            )
            both = both[:rows] + both[rows:]
            tile = jnp.zeros((npc, nk * npv), jnp.float32)
            for k in range(nk):
                tile = jnp.where(lane == k, both[k * npc : (k + 1) * npc], tile)
            part[n * X + i] = tile
        for i in range(X):
            to_p = p_of(i, row)
            to_j = j_of(1, to_p // CORES, lax.rem(to_p, CORES))

            @pl.when(to_j == me_j)
            def _():
                pltpu.make_async_copy(part.at[n * X + i], tiles.at[me_j], tile_sem).start()

            @pl.when(to_j != me_j)
            def _():
                send(part.at[n * X + i], tiles.at[me_j], sent_sem.at[4], tile_sem, me_p, to_j)

    adds_for = y * CORES + core

    def add_up(row):
        @pl.when((zl == 1) & (lax.rem(adds_for, ZH) == row))
        def _():
            wait(tiles, tile_sem)
            sums = [tiles[j] for j in range(NJ)]
            while len(sums) > 1:
                sums = [a + b for a, b in zip(sums[::2], sums[1::2])] + sums[len(sums) // 2 * 2 :]
            total[...] = sums[0]

            @pl.loop(0, NJ)
            def _(j):
                itself = (adds_for == me_p) & (j == me_j)

                @pl.when(itself)
                def _():
                    pltpu.make_async_copy(total, back.at[me_p], back_sem).start()

                @pl.when(jnp.logical_not(itself))
                def _():
                    send(total, back.at[me_p], sent_sem.at[5], back_sem, adds_for, j)

    def screened_ready():
        wait(wt_pair, wt_pair_sem)

    for step in (
        (begin, 0), (prepare, 0), (begin, 1), (prepare, 1), (enter, 0), (begin, 3), (prepare, 2), (enter, 1), (begin, 2),
        (prepare, 3), (enter, 3), (prepare, 4), (enter, 2), (valence_out,), (prepare, 5), (screened_out,), (labels,),
        (hop, 0, 1), (hop, 1, 1), (hop, 2, 1), (hop, 3, 1), (screened_ready,),
        (hop, 0, 2), (multiply, 0, 0), (multiply, 1, 0), (hop, 1, 2), (multiply, 2, 0), (multiply, 3, 0), (hop, 2, 2),
        (multiply, 0, 1), (hop, 3, 2), (multiply, 1, 1), (hop, 0, 3), (multiply, 2, 1), (multiply, 3, 1), (hop, 1, 3),
        (multiply, 0, 2), (multiply, 1, 2), (hop, 2, 3), (multiply, 2, 2), (hop, 3, 3), (multiply, 3, 2), (valence_pair, 0),
        (valence_pair, 1), (valence_pair, 2), (valence_pair, 3), (hop, 0, 4),
        (multiply, 0, 3), (multiply, 0, 4), (second, 0), (hop, 1, 4), (multiply, 1, 3), (multiply, 1, 4), (second, 1),
        (hop, 2, 4), (multiply, 2, 3), (multiply, 2, 4), (second, 2), (hop, 3, 4), (multiply, 3, 3), (multiply, 3, 4),
        (second, 3), (add_up, 0), (add_up, 1), (add_up, 2), (add_up, 3),
    ):
        step[0](*step[1:])

    wait(back, back_sem)
    for j in range(NP):
        chosen = jnp.zeros((npc, nk * npv), jnp.float32)
        for q in range(NP):
            chosen = jnp.where(label[q] == j, back[q], chosen)
        for k in range(nk):
            out_ref[k, j] = chosen[:, k * npv : (k + 1) * npv]

    hops = sum(REACH_UP + REACH_DOWN) * ZL + (ZL - 1) * ZH
    wait(con_in.at[pl.ds(0, NP - 1)], sent_sem.at[0])
    wait(wide.at[pl.ds(0, hops)], sent_sem.at[1])
    wait(val_in, sent_sem.at[2])
    wait(val_in.at[pl.ds(0, NP - 1)], sent_sem.at[3])
    wait(wt_pair, sent_sem.at[6])

    @pl.when(zl == 1)
    def _():
        wait(part.at[pl.ds(0, NP - 1)], sent_sem.at[4])

        @pl.when(adds_for == me_p)
        def _():
            wait(tiles.at[pl.ds(0, NJ - 1)], sent_sem.at[5])

        @pl.when(adds_for != me_p)
        def _():
            wait(tiles, sent_sem.at[5])

    @pl.when(zl != 1)
    def _():
        wait(part, sent_sem.at[4])


def per_device(valence, conduction, screened, kq_table):
    nk, nq, npv, own = valence.shape
    npc = conduction.shape[2]
    rows = nk * npc
    return pl.pallas_call(
        kernel,
        out_shape=jax.ShapeDtypeStruct((nk, nq, npc, npv), jnp.float32),
        in_specs=[pl.BlockSpec(memory_space=pltpu.HBM)] * 4,
        out_specs=pl.BlockSpec(memory_space=pltpu.VMEM),
        scratch_shapes=[
            pltpu.VMEM((NP, nk, npc, own), jnp.bfloat16),
            pltpu.VMEM((NP, nk, npv, own), jnp.bfloat16),
            pltpu.VMEM((NP, nk, npv, own), jnp.bfloat16),
            pltpu.VMEM((NS * ZH, (X - 1) * rows, 128), jnp.bfloat16),
            pltpu.VMEM((own, NJ * own), jnp.bfloat16),
            pltpu.SMEM((nk, nq), jnp.int32),
            pltpu.VMEM((NJ, own, 128), jnp.bfloat16),
            pltpu.VMEM((NS, own, 128), jnp.bfloat16),
            pltpu.VMEM((ZH, X * rows, 256), jnp.float32),
            pltpu.VMEM((NP, npc, nk * npv), jnp.float32),
            pltpu.VMEM((NJ, npc, nk * npv), jnp.float32),
            pltpu.VMEM((npc, nk * npv), jnp.float32),
            pltpu.VMEM((NP, npc, nk * npv), jnp.float32),
            pltpu.VMEM((NP, npc, nk * npv), jnp.int32),
            pltpu.SemaphoreType.DMA((ZH,)),
            pltpu.SemaphoreType.DMA((ZH,)),
            pltpu.SemaphoreType.DMA((ZH,)),
            pltpu.SemaphoreType.DMA,
            pltpu.SemaphoreType.DMA((NS * ZH,)),
            pltpu.SemaphoreType.DMA,
            pltpu.SemaphoreType.DMA,
            pltpu.SemaphoreType.DMA((7,)),
            pltpu.SemaphoreType.DMA((2,)),
        ],
        compiler_params=pltpu.CompilerParams(collective_id=0, has_side_effects=True, vmem_limit_bytes=67043328),
    )(valence, conduction, screened, kq_table)


def solution(mesh):
    return jax.shard_map(
        per_device,
        mesh=mesh,
        in_specs=(
            P("pb", None, None, "ga"),
            P("pb", None, None, "ga"),
            P("pb", "ga", None),
            P("pb", None),
        ),
        out_specs=P("pb", None, None, None),
        check_vma=False,
    )
```

```python
import jax
import jax.numpy as jnp
from jax import lax
from jax.experimental import pallas as pl
from jax.experimental.pallas import tpu as pltpu
from jax.sharding import PartitionSpec as P

MESH = pl.DeviceIdType.MESH
X, ZH, ZL, Y, CORES = 4, 4, 3, 8, 2
NP, NJ = X * ZH, ZL * Y * CORES
NS = ZL * Y
REACH_UP = (4, 3, 3, 4)
REACH_DOWN = (3, 4, 4, 3)
PREPARE = 6


def kernel(
    val_ref, con_ref, w_hbm, table_hbm, out_ref,
    con_in, val_in, val_pair, wide, w_ref, table_ref, wt, wt_pair, acc, part, tiles, total, back, label,
    con_sem, val_sem, val_pair_sem, wt_pair_sem, hop_sem, tile_sem, back_sem, sent_sem, load_sem,
):
    me_p, me_j = lax.axis_index("pb"), lax.axis_index("ga")
    x, zh = me_p // ZH, lax.rem(me_p, ZH)
    zl, y, core = me_j // (Y * CORES), lax.rem(me_j // CORES, Y), lax.rem(me_j, CORES)
    nk, _, npc, own = con_ref.shape
    npv = val_ref.shape[2]
    rows = nk * npc
    spare = 128 - own

    def p_of(px, pz):
        return px * ZH + lax.rem(pz, ZH)

    def j_of(jz, jy, jc):
        return (lax.rem(jz, ZL) * Y + lax.rem(jy, Y)) * CORES + jc

    def slot_of(sy, sz, n):
        return (lax.rem(sy, Y) * ZL + lax.rem(sz, ZL)) * ZH + n

    def send(src, dst, sent, arrived, p, j):
        pltpu.make_async_remote_copy(
            src_ref=src, dst_ref=dst, send_sem=sent, recv_sem=arrived, device_id=(p, j), device_id_type=MESH
        ).start()

    def wait(ref, sem):
        pltpu.make_async_copy(ref, ref, sem).wait()

    pair = j_of(zl, y, 1 - core)
    load_w = pltpu.make_async_copy(w_hbm.at[0], w_ref, load_sem.at[0])
    load_table = pltpu.make_async_copy(table_hbm, table_ref, load_sem.at[1])
    load_w.start()
    load_table.start()

    barrier = pltpu.get_barrier_semaphore()
    near = [(p_of(lax.rem(x + dx, X), zh + d), me_j) for d in range(ZH) for dx in range(X) if d or dx]
    near += [(me_p, j_of(zl + d, y, core)) for d in range(1, ZL)]
    near += [(me_p, j_of(zl, y + d, core)) for d in (1, Y - 1)] + [(me_p, pair)]
    for p, j in near:
        pl.semaphore_signal(barrier, inc=1, device_id=(p, j), device_id_type=MESH)
    pl.semaphore_wait(barrier, len(near))

    def exchange(ref, into, sent, sem, d):
        slot = (ZH - d) % ZH * X + x
        for dx in range(X):
            to = p_of(lax.rem(x + dx, X), zh + d)
            if d or dx:
                send(ref.at[:, to], into.at[slot], sent_sem.at[sent], sem.at[(ZH - d) % ZH], to, me_j)
            else:
                pltpu.make_async_copy(ref.at[:, to], into.at[slot], sem.at[0]).start()

    for d in (0, 1, 3, 2):
        exchange(con_ref, con_in, 0, con_sem, d)

    def valence_out():
        for d in (0, 1, 3, 2):
            exchange(val_ref, val_in, 3, val_sem, d)

    def prepare(piece):
        if piece == 0:
            load_w.wait()
        tiles_each = w_ref.shape[1] // 128 // PREPARE

        @pl.loop(piece * tiles_each, (piece + 1) * tiles_each)
        def _(a):
            at = pl.multiple_of(a * 128, 128)
            block = w_ref[:, pl.ds(at, 128)].astype(jnp.float32)
            block = jnp.concatenate([block, jnp.zeros((spare, 128), jnp.float32)], axis=0).T.astype(jnp.bfloat16)
            for b in range(128 // 32):
                row = a * (128 // 32) + b
                wt[row // (own // 32), pl.ds(pl.multiple_of(lax.rem(row, own // 32) * 32, 32), 32), :] = block[32 * b : 32 * b + 32]

    def screened_out():
        by_core = wt.reshape(NS, CORES, own, 128)
        send(by_core.at[:, 1 - core], wt_pair, sent_sem.at[6], wt_pair_sem, me_p, pair)

    def labels():
        load_table.wait()
        lane = lax.broadcasted_iota(jnp.int32, (npc, nk * npv), 1) // npv
        for q in range(NP):
            value = jnp.zeros((npc, nk * npv), jnp.int32)
            for k in range(nk):
                value = jnp.where(lane == k, table_ref[k, q], value)
            label[q] = value

    def onward(slot, up, down):
        for go, d in ((up, 1), (down, Y - 1)):
            if go:
                send(wide.at[slot], wide.at[slot], sent_sem.at[1], hop_sem.at[slot], me_p, j_of(zl, y + d, core))

    def begin(n):
        slot = slot_of(y, zl, n)
        wait(con_in.at[pl.ds(n * X, X)], con_sem.at[n])
        parts = [con_in[n * X + i].astype(jnp.float32).reshape(rows, own) for i in range(X)]
        for i in range(X - 1):
            packed = jnp.concatenate([parts[i], parts[X - 1][:, spare * i : spare * (i + 1)]], axis=1)
            wide[slot, i * rows : (i + 1) * rows, :] = packed.astype(jnp.bfloat16)
        for d in range(1, ZL):
            send(wide.at[slot], wide.at[slot], sent_sem.at[1], hop_sem.at[slot], me_p, j_of(zl + d, y, core))
        onward(slot, True, True)

    def enter(n):
        for dz in range(1, ZL):
            slot = slot_of(y, zl + dz, n)
            wait(wide.at[slot], hop_sem.at[slot])
            onward(slot, True, True)

    def offset(row):
        return lax.rem(row + ZH - zh, ZH)

    def hop(row, t):
        for dz in range(ZL):
            for sy, reach, up in ((y + Y - t, REACH_UP[row], True), (y + t, REACH_DOWN[row], False)):
                if t <= reach:
                    slot = slot_of(sy, zl + dz, offset(row))
                    wait(wide.at[slot], hop_sem.at[slot])
                    onward(slot, up and t < reach, not up and t < reach)

    def multiply(row, t):
        n = offset(row)
        for sy in [y + t] if t in (0, Y // 2) else [y + Y - t, y + t]:
            left, right = [], []
            for z in range(ZL):
                chunk = wide[slot_of(sy, z, n)]
                thirds = [chunk[i * rows : (i + 1) * rows].astype(jnp.float32) for i in range(X - 1)]
                fourth = jnp.concatenate([third[:, own:] for third in thirds] + [thirds[0][:, own:]], axis=1)
                left.append(jnp.concatenate([chunk, fourth.astype(jnp.bfloat16)], axis=0))
                source = z * Y + lax.rem(sy, Y)
                both = jnp.concatenate([wt[source * CORES + core], wt_pair[source]], axis=1)
                right += [both, jnp.zeros((spare, 256), jnp.bfloat16)]
            product = jnp.dot(
                jnp.concatenate(left, axis=1), jnp.concatenate(right, axis=0), preferred_element_type=jnp.float32
            )
            acc[n] = product if t == 0 else acc[n] + product

    def valence_pair(row):
        n = offset(row)
        here = pl.ds(n * X, X)
        wait(val_in.at[here], val_sem.at[n])
        send(val_in.at[here], val_pair.at[here], sent_sem.at[2], val_pair_sem.at[n], me_p, pair)

    def second(row):
        n = offset(row)
        wait(val_pair.at[pl.ds(n * X, X)], val_pair_sem.at[n])
        lane = lax.broadcasted_iota(jnp.int32, (npc, nk * npv), 1) // npv
        for i in range(X):
            u = acc[n, i * rows : (i + 1) * rows, :]
            high = u.astype(jnp.bfloat16)
            low = (u - high.astype(jnp.float32)).astype(jnp.bfloat16)
            stacked = jnp.concatenate([high, low], axis=0)
            both = sum(
                lax.dot_general(
                    stacked[:, at : at + own], from_[n * X + i].reshape(nk * npv, own),
                    (((1,), (1,)), ((), ())), preferred_element_type=jnp.float32,
                )
                for at, from_ in ((0, val_in), (128, val_pair))
            )
            both = both[:rows] + both[rows:]
            tile = jnp.zeros((npc, nk * npv), jnp.float32)
            for k in range(nk):
                tile = jnp.where(lane == k, both[k * npc : (k + 1) * npc], tile)
            part[n * X + i] = tile
        for i in range(X):
            to_p = p_of(i, row)
            to_j = j_of(1, to_p // CORES, lax.rem(to_p, CORES))

            @pl.when(to_j == me_j)
            def _():
                pltpu.make_async_copy(part.at[n * X + i], tiles.at[me_j], tile_sem).start()

            @pl.when(to_j != me_j)
            def _():
                send(part.at[n * X + i], tiles.at[me_j], sent_sem.at[4], tile_sem, me_p, to_j)

    adds_for = y * CORES + core

    def add_up(row):
        @pl.when((zl == 1) & (lax.rem(adds_for, ZH) == row))
        def _():
            wait(tiles, tile_sem)
            sums = [tiles[j] for j in range(NJ)]
            while len(sums) > 1:
                sums = [a + b for a, b in zip(sums[::2], sums[1::2])] + sums[len(sums) // 2 * 2 :]
            total[...] = sums[0]

            @pl.loop(0, NJ)
            def _(j):
                itself = (adds_for == me_p) & (j == me_j)

                @pl.when(itself)
                def _():
                    pltpu.make_async_copy(total, back.at[me_p], back_sem).start()

                @pl.when(jnp.logical_not(itself))
                def _():
                    send(total, back.at[me_p], sent_sem.at[5], back_sem, adds_for, j)

    def screened_ready():
        wait(wt_pair, wt_pair_sem)

    for step in (
        (begin, 0), (begin, 1), (enter, 0), (begin, 3), (enter, 1), (begin, 2), (prepare, 0),
        (enter, 3), (prepare, 1), (enter, 2), (prepare, 2), (prepare, 3), (prepare, 4), (prepare, 5), (screened_out,), (labels,),
        (hop, 0, 1), (hop, 1, 1), (hop, 2, 1), (hop, 3, 1), (valence_out,), (screened_ready,),
        (hop, 0, 2), (multiply, 0, 0), (multiply, 1, 0), (hop, 1, 2), (multiply, 2, 0), (multiply, 3, 0), (hop, 2, 2),
        (multiply, 0, 1), (hop, 3, 2), (multiply, 1, 1), (hop, 0, 3), (multiply, 2, 1), (multiply, 3, 1), (hop, 1, 3),
        (multiply, 0, 2), (multiply, 1, 2), (hop, 2, 3), (multiply, 2, 2), (hop, 3, 3), (multiply, 3, 2), (valence_pair, 0),
        (valence_pair, 1), (valence_pair, 2), (valence_pair, 3), (hop, 0, 4),
        (multiply, 0, 3), (multiply, 0, 4), (second, 0), (hop, 1, 4), (multiply, 1, 3), (multiply, 1, 4), (second, 1),
        (hop, 2, 4), (multiply, 2, 3), (multiply, 2, 4), (second, 2), (hop, 3, 4), (multiply, 3, 3), (multiply, 3, 4),
        (second, 3), (add_up, 0), (add_up, 1), (add_up, 2), (add_up, 3),
    ):
        step[0](*step[1:])

    wait(back, back_sem)
    for j in range(NP):
        chosen = jnp.zeros((npc, nk * npv), jnp.float32)
        for q in range(NP):
            chosen = jnp.where(label[q] == j, back[q], chosen)
        for k in range(nk):
            out_ref[k, j] = chosen[:, k * npv : (k + 1) * npv]

    hops = sum(REACH_UP + REACH_DOWN) * ZL + (ZL - 1) * ZH
    wait(con_in.at[pl.ds(0, NP - 1)], sent_sem.at[0])
    wait(wide.at[pl.ds(0, hops)], sent_sem.at[1])
    wait(val_in, sent_sem.at[2])
    wait(val_in.at[pl.ds(0, NP - 1)], sent_sem.at[3])
    wait(wt_pair, sent_sem.at[6])

    @pl.when(zl == 1)
    def _():
        wait(part.at[pl.ds(0, NP - 1)], sent_sem.at[4])

        @pl.when(adds_for == me_p)
        def _():
            wait(tiles.at[pl.ds(0, NJ - 1)], sent_sem.at[5])

        @pl.when(adds_for != me_p)
        def _():
            wait(tiles, sent_sem.at[5])

    @pl.when(zl != 1)
    def _():
        wait(part, sent_sem.at[4])


def per_device(valence, conduction, screened, kq_table):
    nk, nq, npv, own = valence.shape
    npc = conduction.shape[2]
    rows = nk * npc
    return pl.pallas_call(
        kernel,
        out_shape=jax.ShapeDtypeStruct((nk, nq, npc, npv), jnp.float32),
        in_specs=[pl.BlockSpec(memory_space=pltpu.HBM)] * 4,
        out_specs=pl.BlockSpec(memory_space=pltpu.VMEM),
        scratch_shapes=[
            pltpu.VMEM((NP, nk, npc, own), jnp.bfloat16),
            pltpu.VMEM((NP, nk, npv, own), jnp.bfloat16),
            pltpu.VMEM((NP, nk, npv, own), jnp.bfloat16),
            pltpu.VMEM((NS * ZH, (X - 1) * rows, 128), jnp.bfloat16),
            pltpu.VMEM((own, NJ * own), jnp.bfloat16),
            pltpu.SMEM((nk, nq), jnp.int32),
            pltpu.VMEM((NJ, own, 128), jnp.bfloat16),
            pltpu.VMEM((NS, own, 128), jnp.bfloat16),
            pltpu.VMEM((ZH, X * rows, 256), jnp.float32),
            pltpu.VMEM((NP, npc, nk * npv), jnp.float32),
            pltpu.VMEM((NJ, npc, nk * npv), jnp.float32),
            pltpu.VMEM((npc, nk * npv), jnp.float32),
            pltpu.VMEM((NP, npc, nk * npv), jnp.float32),
            pltpu.VMEM((NP, npc, nk * npv), jnp.int32),
            pltpu.SemaphoreType.DMA((ZH,)),
            pltpu.SemaphoreType.DMA((ZH,)),
            pltpu.SemaphoreType.DMA((ZH,)),
            pltpu.SemaphoreType.DMA,
            pltpu.SemaphoreType.DMA((NS * ZH,)),
            pltpu.SemaphoreType.DMA,
            pltpu.SemaphoreType.DMA,
            pltpu.SemaphoreType.DMA((7,)),
            pltpu.SemaphoreType.DMA((2,)),
        ],
        compiler_params=pltpu.CompilerParams(collective_id=0, has_side_effects=True, vmem_limit_bytes=67043328),
    )(valence, conduction, screened, kq_table)


def solution(mesh):
    return jax.shard_map(
        per_device,
        mesh=mesh,
        in_specs=(
            P("pb", None, None, "ga"),
            P("pb", None, None, "ga"),
            P("pb", "ga", None),
            P("pb", None),
        ),
        out_specs=P("pb", None, None, None),
        check_vma=False,
    )
```
